32 devices in a mesh: seq: 8 (over z, y), pack: 4 (over x, core).
Axes of the slice: x: 2, y: 2, z: 4, core: 2. Of those that a mesh axis runs over, the one named last changes fastest.
Arguments:
- queries: bfloat16 [8192, 2048], P(('pack', 'seq')), parts along dimension 0, may hold values from -10 to 10
- keys: bfloat16 [8192, 512], P(('pack', 'seq')), parts along dimension 0, may hold values from -10 to 10
- values: bfloat16 [8192, 512], P(('pack', 'seq')), parts along dimension 0, may hold values from -6 to 6
- lengths: int32 [32], P('pack'), parts along dimension 0, may hold values from 1 to 1024, 2048 in all
- home: int32 [64], P('pack'), parts along dimension 0, may hold values from 0 to 7, as said below
Outputs:
- attended: bfloat16 [8192, 2048], P(('pack', 'seq')), parts along dimension 0
The draws below stay inside these ranges and needn't reach their ends.
There are 4 independent parts, one for each index of `pack`. The reference program is written for one: setup_inputs(seed, part) draws one part's arguments, and reference() takes and returns one part's arrays. A program takes and returns all parts, laid end to end along the dimension named above; each array names one. Nothing has to cross between parts.
Inputs may be any that keep to these rules, and one draw needn't show every extreme that they name: Block b covers positions b * 128 to b * 128 + 127. home[b] is 2 * (b // 4) or that plus one, and every device index is home of exactly 2 blocks.
All inputs are finite; a program needn't handle non-finite values.
Results may differ from the reference program's by a relative error of at most 0.0033.
Values may be sent and summed in bfloat16 or wider, within the bound.
A program may use at most 64 MiB of HBM per device.

```python
import math
import jax
import jax.numpy as jnp
import numpy as np
from jax import lax

QH = 16
KVH = 4
HD = 128
BLOCK = 128
GROUP = 4
WINDOW = 2048
TOKENS = 2048
DOCS = 8
MOST_LEN = 1024
NBLK = 16
BPD = 2


def draw_queries(key, part):
    normal_part = jnp.clip(jax.random.normal(jax.random.fold_in(key, 11), (TOKENS, QH * HD), jnp.float32), -6.0, 6.0)
    return normal_part.astype(jnp.bfloat16)


def draw_keys(key, part):
    normal_part = jnp.clip(jax.random.normal(jax.random.fold_in(key, 12), (TOKENS, KVH * HD), jnp.float32), -6.0, 6.0)
    return normal_part.astype(jnp.bfloat16)


def draw_home(key, part):
    group_count = NBLK // (2 * BPD)
    group_keys = jax.random.split(jax.random.fold_in(key, 21), group_count)
    shuffles = jax.vmap(lambda one_key: jax.random.permutation(one_key, 2 * BPD))(group_keys)
    ranking = jnp.argsort(shuffles, axis=1, stable=True).astype(jnp.int32)
    group_ids = jnp.arange(group_count, dtype=jnp.int32)[:, None]
    home = 2 * group_ids + (ranking >= BPD).astype(jnp.int32)
    return home.reshape(NBLK).astype(jnp.int32)


def block_levels(key, dims, shards, least, top_value):
    def one(axis_at, shards_of):
        heights = jax.random.uniform(jax.random.fold_in(jax.random.fold_in(key, 6), axis_at), (shards_of,), jnp.float32, least / len(shards), top_value / len(shards))
        return jnp.repeat(jnp.exp(heights), dims[axis_at] // shards_of).reshape((-1,) + (1,) * (len(dims) - axis_at - 1))

    level = one(*shards[0])
    for cut in shards[1:]:
        level = level * one(*cut)
    return level


def split_up(amount, total, reach, lean):
    weights = [(1 << 20) // math.isqrt(standing ** lean) + 1 for standing in range(2, amount + 1)]
    rest, counts = total - reach - (amount - 1), [1] * (amount - 1)
    while rest > 0:
        movable = [i for i in range(amount - 1) if counts[i] < reach]
        pool, left = sum([weights[i] for i in movable]), rest
        for i in movable:
            extra = min(reach - counts[i], max(1, left * weights[i] // pool), rest)
            counts[i] = counts[i] + extra
            rest = rest - extra
    return np.array([reach] + counts)


def uneven(stream_key, count, total, bound, skew):
    if count == 2:
        one = jax.random.randint(stream_key, (), max(1, total - bound), min(bound, total - 1) + 1)
        return jnp.stack([one, total - one])
    sizes = jnp.asarray(split_up(count, total, bound, skew), jnp.int32)
    twos = (count - 1) // 2
    giver, taker = sizes[1:1 + 2 * twos:2], sizes[2:2 + 2 * twos:2]
    margin = jnp.minimum(giver - 1, bound - taker)
    moved = jax.random.randint(jax.random.fold_in(stream_key, 1), (twos,), 0, 1 << 20) % (margin + 1)
    sizes = sizes.at[1:1 + 2 * twos:2].set(giver - moved).at[2:2 + 2 * twos:2].set(taker + moved)
    return sizes[jax.random.permutation(jax.random.fold_in(stream_key, 2), count)]


def gaussian(own_key, dims, deviation, reach, shards=(), kind=jnp.bfloat16):
    drawn = jax.random.normal(own_key, dims, jnp.float32) * deviation
    if len(shards) > 0:
        drawn = block_levels(own_key, dims, shards, -0.22, 0.18) * drawn
    return jnp.clip(drawn, min=-reach, max=reach).astype(kind)


def setup_inputs(seed: int = 0, part: int = 0) -> dict:
    arg_keys = jax.random.split(jax.random.key(seed), 6)
    part_keys = jax.random.split(jax.random.fold_in(arg_keys[5], part), 6)
    queries = draw_queries(jax.random.fold_in(jax.random.fold_in(arg_keys[5], part), 71), part)
    keys = draw_keys(jax.random.fold_in(jax.random.fold_in(arg_keys[5], part), 71), part)
    values = gaussian(part_keys[2], (TOKENS, KVH * HD), 1.0, 6.0, ((0, 8),))
    lengths = uneven(part_keys[3], DOCS, TOKENS, MOST_LEN, 2).astype(jnp.int32)
    home = draw_home(jax.random.fold_in(jax.random.fold_in(arg_keys[5], part), 71), part)
    return dict(queries=queries, keys=keys, values=values, lengths=lengths, home=home)


def doc_first_of(lengths, positions):
    doc_ends = jnp.cumsum(lengths).astype(jnp.int32)
    doc_starts = (doc_ends - lengths).astype(jnp.int32)
    chosen = jnp.where(doc_starts[None, :] <= positions[:, None], doc_starts[None, :], 0)
    return jnp.max(chosen, axis=1).astype(jnp.int32)


def reference(queries, keys, values, lengths, home):
    positions = jnp.arange(TOKENS, dtype=jnp.int32)
    doc_first = doc_first_of(lengths, positions)
    zero_rows = jnp.zeros((WINDOW, KVH * HD), jnp.bfloat16)
    keys_padded = jnp.concatenate([zero_rows, keys], axis=0)
    values_padded = jnp.concatenate([zero_rows, values], axis=0)

    def one_block(block_id):
        row_start = (block_id * BLOCK).astype(jnp.int32)
        query_rows = lax.dynamic_slice_in_dim(queries, row_start, BLOCK, 0).astype(jnp.float32).reshape(BLOCK, KVH, GROUP, HD)
        key_rows = lax.dynamic_slice_in_dim(keys_padded, row_start, WINDOW + BLOCK, 0).astype(jnp.float32).reshape(WINDOW + BLOCK, KVH, HD)
        value_rows = lax.dynamic_slice_in_dim(values_padded, row_start, WINDOW + BLOCK, 0).astype(jnp.float32).reshape(WINDOW + BLOCK, KVH, HD)
        query_pos = row_start + jnp.arange(BLOCK, dtype=jnp.int32)
        key_pos = row_start - WINDOW + jnp.arange(WINDOW + BLOCK, dtype=jnp.int32)
        first_rows = lax.dynamic_slice_in_dim(doc_first, row_start, BLOCK, 0)
        allowed = (key_pos[None, :] <= query_pos[:, None]) & (key_pos[None, :] > query_pos[:, None] - WINDOW) & (key_pos[None, :] >= first_rows[:, None])
        scores = jnp.einsum("qhgd,khd->hgqk", query_rows, key_rows) * (HD ** -0.5)
        scores = jnp.where(allowed, scores, jnp.float32(-1e30))
        row_max = jnp.max(scores, axis=-1, keepdims=True)
        weights = jnp.where(allowed, jnp.exp(scores - row_max), jnp.float32(0.0))
        denominator = jnp.sum(weights, axis=-1)
        rounded = lax.optimization_barrier(weights.astype(jnp.bfloat16)).astype(jnp.float32)
        numerator = jnp.einsum("hgqk,khd->hgqd", rounded, value_rows)
        mixed = numerator / denominator[..., None]
        return mixed.transpose(2, 0, 1, 3).reshape(BLOCK, QH * HD).astype(jnp.bfloat16)

    block_outputs = lax.map(one_block, jnp.arange(NBLK, dtype=jnp.int32))
    slot_order = jnp.argsort(home, stable=True).astype(jnp.int32)
    return block_outputs[slot_order].reshape(TOKENS, QH * HD)
```

```python
import functools

import jax
import jax.numpy as jnp
from jax import lax
from jax.experimental import pallas as pl
from jax.experimental.pallas import tpu as pltpu
from jax.sharding import PartitionSpec as P

HD = 128
BLOCK = 128
WINDOW = 2048
LOG2E = 1.4426950408889634


def hop_back(value, pairs):
    count = lax.axis_size("seq")
    return lax.ppermute(
        value, "seq", [(source, source + 2 * pairs) for source in range(count - 2 * pairs)]
    )


def swap(value):
    count = lax.axis_size("seq")
    return lax.ppermute(value, "seq", [(source, source ^ 1) for source in range(count)])


def doc_first_of(lengths, positions):
    doc_ends = jnp.cumsum(lengths)
    doc_starts = doc_ends - lengths
    chosen = jnp.where(doc_starts[None, :] <= positions[:, None], doc_starts[None, :], 0)
    return jnp.max(chosen, axis=1)


def attend(
    group, bases, slots, firsts, blocks, lows, own_queries, other_queries, *rest
):
    pieces, (out, top, total, mixed) = rest[:-4], rest[-4:]
    scale = HD ** (-0.5) * LOG2E
    rows = own_queries.shape[0]
    for block in range(2 * rows // BLOCK):
        side, inner = block // (rows // BLOCK), block % (rows // BLOCK)
        source = own_queries if side == 0 else other_queries
        here = pl.ds(inner * BLOCK, BLOCK)
        first = bases[side] + inner * BLOCK
        lowest = firsts[block]
        low = lows[pl.ds(block * BLOCK, BLOCK), :]

        def scored(piece, base):
            grouped = jnp.concatenate(
                [source[here, pl.ds(g * HD, HD)] for g in range(group)], axis=0
            )
            keys = piece[0]
            count = keys.shape[0]
            raw = lax.dot_general(
                grouped, keys, (((1,), (1,)), ((), ())), preferred_element_type=jnp.float32
            )
            key_pos = base + lax.broadcasted_iota(jnp.int32, (BLOCK, count), 1)
            query_pos = first + lax.broadcasted_iota(jnp.int32, (BLOCK, count), 0)
            low_wide = jnp.concatenate([low] * (count // HD), axis=1)
            allowed = (key_pos <= query_pos) & (key_pos >= low_wide)
            shaped = raw.reshape(group, BLOCK, count) * scale
            return jnp.where(allowed[None], shaped, -1e30).reshape(group * BLOCK, count)

        def folded(piece, weights):
            return jnp.dot(
                weights.astype(jnp.bfloat16), piece[1], preferred_element_type=jnp.float32
            )

        order = [side] + [i for i in range(len(pieces)) if i != side]
        for place, index in enumerate(order):
            piece, base = pieces[index], bases[index]
            count = piece.shape[1]
            if place == 0:
                scores = scored(piece, base)
                peak = jnp.max(scores, axis=1, keepdims=True)
                weights = jnp.exp2(scores - peak)
                top[...] = jnp.broadcast_to(peak, top.shape)
                total[...] = jnp.broadcast_to(
                    jnp.sum(weights, axis=1, keepdims=True), total.shape
                )
                mixed[...] = folded(piece, weights)
                continue

            @pl.when((base <= first) & (base + count > lowest))
            def _():
                scores = scored(piece, base)
                before = top[...]
                peak = jnp.maximum(before, jnp.max(scores, axis=1, keepdims=True))
                weights = jnp.exp2(scores - jnp.concatenate([peak] * (count // HD), axis=1))
                rescale = jnp.exp2(before - peak)
                top[...] = peak
                total[...] = total[...] * rescale + jnp.sum(weights, axis=1, keepdims=True)
                mixed[...] = mixed[...] * rescale + folded(piece, weights)

        result = (mixed[...] / total[...]).astype(out.dtype)
        slot = slots[block]
        for g in range(group):
            out[slot, :, pl.ds(g * HD, HD)] = result[g * BLOCK : (g + 1) * BLOCK]


def attention(group, scalars, lows, own_queries, other_queries, pieces, blocks):
    rows = own_queries.shape[0]
    vmem = pl.BlockSpec(memory_space=pltpu.VMEM)
    smem = pl.BlockSpec(memory_space=pltpu.SMEM)
    operands = (*scalars, lows, own_queries, other_queries, *pieces)
    tall = (group * BLOCK, HD)
    keys_seen = len(pieces) * rows
    return pl.pallas_call(
        functools.partial(attend, group),
        out_shape=jax.ShapeDtypeStruct((blocks, BLOCK, group * HD), jnp.bfloat16),
        in_specs=[smem] * len(scalars) + [vmem] * (len(operands) - len(scalars)),
        out_specs=vmem,
        scratch_shapes=[pltpu.VMEM(tall, jnp.float32)] * 3,
        compiler_params=pltpu.CompilerParams(vmem_limit_bytes=24 * 1024 * 1024),
        cost_estimate=pl.CostEstimate(
            flops=4 * blocks * BLOCK * group * HD * keys_seen // 2,
            bytes_accessed=4 * rows * group * HD * 4,
            transcendentals=blocks * BLOCK * group * keys_seen // 2,
        ),
    )(*operands)


def local(queries, keys, values, lengths, home):
    rows, query_cols = queries.shape
    kv_heads = keys.shape[1] // HD
    group = query_cols // HD // kv_heads
    half_heads = kv_heads // 2
    blocks_dev = rows // BLOCK
    blocks = 2 * blocks_dev
    seq = lax.axis_size("seq")
    tokens = seq * rows
    most_len = min(tokens // 2, 4096)
    depth = min(-(-(min(WINDOW, most_len) - 1) // (2 * rows)), seq // 2 - 1)
    me = lax.axis_index("seq")
    other = me ^ 1
    parity = me % 2

    def halves(array):
        width = array.shape[1] // 2
        low, high = array[:, :width], array[:, width:]
        return jnp.where(parity == 0, low, high), jnp.where(parity == 0, high, low)

    def by_head(array):
        return [array[:, h * HD : (h + 1) * HD] for h in range(half_heads)]

    keys_mine, keys_give = halves(keys)
    values_mine, values_give = halves(values)
    own_kv = [jnp.stack(kv) for kv in zip(by_head(keys_mine), by_head(values_mine))]
    give_kv = [jnp.stack(kv) for kv in zip(by_head(keys_give), by_head(values_give))]
    queries_mine, queries_give = halves(queries)
    wide = group * HD

    own_pos = me * rows + jnp.arange(rows, dtype=jnp.int32)
    other_pos = other * rows + jnp.arange(rows, dtype=jnp.int32)
    positions = jnp.concatenate([own_pos, other_pos])
    low = jnp.maximum(doc_first_of(lengths, positions), positions - (WINDOW - 1))
    lows = jnp.broadcast_to(low[:, None], (2 * rows, HD))
    firsts = low[::BLOCK]
    bases = jnp.stack(
        [(device - 2 * back) * rows for back in range(depth + 1) for device in (me, other)]
    ).astype(jnp.int32)
    group_home = lax.dynamic_slice_in_dim(home, me // 2 * blocks, blocks, 0)
    same = group_home[:, None] == group_home[None, :]
    earlier = jnp.arange(blocks)[None, :] < jnp.arange(blocks)[:, None]
    rank = jnp.sum((same & earlier).astype(jnp.int32), axis=1)
    slot = jnp.where(group_home == me, rank, blocks_dev + rank).astype(jnp.int32)
    slots = jnp.where(parity == 0, slot, jnp.roll(slot, blocks_dev))
    ids = jnp.arange(blocks, dtype=jnp.int32)

    outs = []
    pieces = []
    asked = []
    for h in range(half_heads):
        mine, theirs = own_kv[h], swap(give_kv[h])
        found = [mine, theirs]
        for _ in range(depth):
            mine, theirs = hop_back(mine, 1), hop_back(theirs, 1)
            found += [mine, theirs]
        pieces.append(found)
        asked.append(swap(queries_give[:, h * wide : (h + 1) * wide]))
    for h in range(half_heads):
        result = attention(
            group,
            (bases, slots, firsts, ids),
            lows,
            queries_mine[:, h * wide : (h + 1) * wide],
            asked[h],
            pieces[h],
            blocks,
        )
        kept = result[:blocks_dev].reshape(rows, wide)
        got = swap(result[blocks_dev:].reshape(rows, wide))
        outs.append((kept, got))
    kept = jnp.concatenate([pair[0] for pair in outs], axis=1)
    got = jnp.concatenate([pair[1] for pair in outs], axis=1)
    return jnp.where(
        parity == 0,
        jnp.concatenate([kept, got], axis=1),
        jnp.concatenate([got, kept], axis=1),
    )


def solution(mesh):
    placed = (
        P(("pack", "seq"), None),
        P(("pack", "seq"), None),
        P(("pack", "seq"), None),
        P("pack"),
        P("pack"),
    )
    return jax.shard_map(
        local, mesh=mesh, in_specs=placed, out_specs=P(("pack", "seq"), None), check_vma=False
    )
```

```python
import functools

import jax
import jax.numpy as jnp
from jax import lax
from jax.experimental import pallas as pl
from jax.experimental.pallas import tpu as pltpu
from jax.sharding import PartitionSpec as P

HD = 128
BLOCK = 128
WINDOW = 2048
LOG2E = 1.4426950408889634


def hop_back(value, pairs):
    count = lax.axis_size("seq")
    return lax.ppermute(
        value, "seq", [(source, source + 2 * pairs) for source in range(count - 2 * pairs)]
    )


def swap(value):
    count = lax.axis_size("seq")
    return lax.ppermute(value, "seq", [(source, source ^ 1) for source in range(count)])


def doc_first_of(lengths, positions):
    doc_ends = jnp.cumsum(lengths)
    doc_starts = doc_ends - lengths
    chosen = jnp.where(doc_starts[None, :] <= positions[:, None], doc_starts[None, :], 0)
    return jnp.max(chosen, axis=1)


def attend(
    group, bases, slots, firsts, blocks, lows, own_queries, other_queries, *rest
):
    pieces, (out, top, total, mixed) = rest[:-4], rest[-4:]
    scale = HD ** (-0.5) * LOG2E
    rows = own_queries.shape[0]
    for side in range(2):
        source = own_queries if side == 0 else other_queries
        first = bases[side]
        lowest = firsts[side * (rows // BLOCK)]
        low = lows[pl.ds(side * rows, rows), :]

        def scored(piece, base):
            grouped = jnp.concatenate(
                [source[:, pl.ds(g * HD, HD)] for g in range(group)], axis=0
            )
            keys = piece[0]
            count = keys.shape[0]
            raw = lax.dot_general(
                grouped, keys, (((1,), (1,)), ((), ())), preferred_element_type=jnp.float32
            )
            key_pos = base + lax.broadcasted_iota(jnp.int32, (rows, count), 1)
            query_pos = first + lax.broadcasted_iota(jnp.int32, (rows, count), 0)
            low_wide = jnp.concatenate([low] * (count // HD), axis=1)
            allowed = (key_pos <= query_pos) & (key_pos >= low_wide)
            shaped = raw.reshape(group, rows, count) * scale
            return jnp.where(allowed[None], shaped, -1e30).reshape(group * rows, count)

        def folded(piece, weights):
            return jnp.dot(
                weights.astype(jnp.bfloat16), piece[1], preferred_element_type=jnp.float32
            )

        def by_lane(weights):
            return sum(weights[:, c : c + HD] for c in range(0, weights.shape[1], HD))

        order = [side] + [i for i in range(len(pieces)) if i != side]
        for place, index in enumerate(order):
            piece, base = pieces[index], bases[index]
            count = piece.shape[1]
            if place == 0:
                scores = scored(piece, base)
                peak = jnp.max(scores, axis=1, keepdims=True)
                weights = jnp.exp2(scores - peak)
                top[...] = jnp.broadcast_to(peak, top.shape)
                total[...] = by_lane(weights)
                mixed[...] = folded(piece, weights)
                continue

            @pl.when((base <= first) & (base + count > lowest))
            def _():
                scores = scored(piece, base)
                before = top[...]
                peak = jnp.maximum(before, jnp.max(scores, axis=1, keepdims=True))
                weights = jnp.exp2(scores - jnp.concatenate([peak] * (count // HD), axis=1))
                rescale = jnp.exp2(before - peak)
                top[...] = peak
                total[...] = total[...] * rescale + by_lane(weights)
                mixed[...] = mixed[...] * rescale + folded(piece, weights)

        summed = jnp.sum(total[...], axis=1, keepdims=True)
        result = (mixed[...] / summed).astype(out.dtype)
        for inner in range(rows // BLOCK):
            slot = slots[side * (rows // BLOCK) + inner]
            for g in range(group):
                start = g * rows + inner * BLOCK
                out[slot, :, pl.ds(g * HD, HD)] = result[start : start + BLOCK]


def attention(group, scalars, lows, own_queries, other_queries, pieces, blocks):
    rows = own_queries.shape[0]
    vmem = pl.BlockSpec(memory_space=pltpu.VMEM)
    smem = pl.BlockSpec(memory_space=pltpu.SMEM)
    operands = (*scalars, lows, own_queries, other_queries, *pieces)
    tall = (group * rows, HD)
    keys_seen = len(pieces) * rows
    return pl.pallas_call(
        functools.partial(attend, group),
        out_shape=jax.ShapeDtypeStruct((blocks, BLOCK, group * HD), jnp.bfloat16),
        in_specs=[smem] * len(scalars) + [vmem] * (len(operands) - len(scalars)),
        out_specs=vmem,
        scratch_shapes=[pltpu.VMEM(tall, jnp.float32)] * 3,
        compiler_params=pltpu.CompilerParams(vmem_limit_bytes=24 * 1024 * 1024),
        cost_estimate=pl.CostEstimate(
            flops=24 * blocks * BLOCK * group * HD * keys_seen // 2,
            bytes_accessed=4 * rows * group * HD * 4,
            transcendentals=blocks * BLOCK * group * keys_seen // 2,
        ),
    )(*operands)


def local(queries, keys, values, lengths, home):
    rows, query_cols = queries.shape
    kv_heads = keys.shape[1] // HD
    group = query_cols // HD // kv_heads
    half_heads = kv_heads // 2
    blocks_dev = rows // BLOCK
    blocks = 2 * blocks_dev
    seq = lax.axis_size("seq")
    tokens = seq * rows
    most_len = min(tokens // 2, 4096)
    depth = min(-(-(min(WINDOW, most_len) - 1) // (2 * rows)), seq // 2 - 1)
    me = lax.axis_index("seq")
    other = me ^ 1
    parity = me % 2

    def halves(array):
        width = array.shape[1] // 2
        low, high = array[:, :width], array[:, width:]
        return jnp.where(parity == 0, low, high), jnp.where(parity == 0, high, low)

    def by_head(array):
        return [array[:, h * HD : (h + 1) * HD] for h in range(half_heads)]

    keys_mine, keys_give = halves(keys)
    values_mine, values_give = halves(values)
    own_kv = [jnp.stack(kv) for kv in zip(by_head(keys_mine), by_head(values_mine))]
    give_kv = [jnp.stack(kv) for kv in zip(by_head(keys_give), by_head(values_give))]
    queries_mine, queries_give = halves(queries)
    wide = group * HD

    own_pos = me * rows + jnp.arange(rows, dtype=jnp.int32)
    other_pos = other * rows + jnp.arange(rows, dtype=jnp.int32)
    positions = jnp.concatenate([own_pos, other_pos])
    low = jnp.maximum(doc_first_of(lengths, positions), positions - (WINDOW - 1))
    lows = jnp.broadcast_to(low[:, None], (2 * rows, HD))
    firsts = low[::BLOCK]
    bases = jnp.stack(
        [(device - 2 * back) * rows for back in range(depth + 1) for device in (me, other)]
    ).astype(jnp.int32)
    group_home = lax.dynamic_slice_in_dim(home, me // 2 * blocks, blocks, 0)
    same = group_home[:, None] == group_home[None, :]
    earlier = jnp.arange(blocks)[None, :] < jnp.arange(blocks)[:, None]
    rank = jnp.sum((same & earlier).astype(jnp.int32), axis=1)
    slot = jnp.where(group_home == me, rank, blocks_dev + rank).astype(jnp.int32)
    slots = jnp.where(parity == 0, slot, jnp.roll(slot, blocks_dev))
    ids = jnp.arange(blocks, dtype=jnp.int32)

    outs = []
    pieces = []
    asked = []
    for h in range(half_heads):
        mine, give = own_kv[h], give_kv[h]
        ask = queries_give[:, h * wide : (h + 1) * wide]
        if h > 0:
            mine, give, ask, _ = lax.optimization_barrier((mine, give, ask, pieces[-1][3]))
        theirs = swap(give)
        found = [mine, theirs]
        for _ in range(depth):
            mine, theirs = hop_back(mine, 1), hop_back(theirs, 1)
            found += [mine, theirs]
        pieces.append(found)
        asked.append(swap(ask))
    for h in range(half_heads):
        result = attention(
            group,
            (bases, slots, firsts, ids),
            lows,
            queries_mine[:, h * wide : (h + 1) * wide],
            asked[h],
            pieces[h],
            blocks,
        )
        kept = result[:blocks_dev].reshape(rows, wide)
        got = swap(result[blocks_dev:].reshape(rows, wide))
        outs.append((kept, got))
    kept = jnp.concatenate([pair[0] for pair in outs], axis=1)
    got = jnp.concatenate([pair[1] for pair in outs], axis=1)
    return jnp.where(
        parity == 0,
        jnp.concatenate([kept, got], axis=1),
        jnp.concatenate([got, kept], axis=1),
    )


def solution(mesh):
    placed = (
        P(("pack", "seq"), None),
        P(("pack", "seq"), None),
        P(("pack", "seq"), None),
        P("pack"),
        P("pack"),
    )
    return jax.shard_map(
        local, mesh=mesh, in_specs=placed, out_specs=P(("pack", "seq"), None), check_vma=False
    )
```

```python
import functools

import jax
import jax.numpy as jnp
from jax import lax
from jax.experimental import pallas as pl
from jax.experimental.pallas import tpu as pltpu
from jax.sharding import PartitionSpec as P

HD = 128
BLOCK = 128
WINDOW = 2048
LOG2E = 1.4426950408889634


def hop_back(value, pairs):
    count = lax.axis_size("seq")
    return lax.ppermute(
        value, "seq", [(source, source + 2 * pairs) for source in range(count - 2 * pairs)]
    )


def swap(value):
    count = lax.axis_size("seq")
    return lax.ppermute(value, "seq", [(source, source ^ 1) for source in range(count)])


def doc_first_of(lengths, positions):
    doc_ends = jnp.cumsum(lengths)
    doc_starts = doc_ends - lengths
    chosen = jnp.where(doc_starts[None, :] <= positions[:, None], doc_starts[None, :], 0)
    return jnp.max(chosen, axis=1)


def attend(
    group, bases, slots, firsts, blocks, lows, own_queries, other_queries, *rest
):
    pieces, (out, top, total, mixed) = rest[:-4], rest[-4:]
    scale = HD ** (-0.5) * LOG2E
    rows = own_queries.shape[0]
    for side in range(2):
        source = own_queries if side == 0 else other_queries
        first = bases[side]
        lowest = firsts[side * (rows // BLOCK)]
        low = lows[pl.ds(side * rows, rows), :]

        def scored(piece, base):
            grouped = jnp.concatenate(
                [source[:, pl.ds(g * HD, HD)] for g in range(group)], axis=0
            )
            keys = piece[0]
            count = keys.shape[0]
            raw = lax.dot_general(
                grouped, keys, (((1,), (1,)), ((), ())), preferred_element_type=jnp.float32
            )
            key_pos = base + lax.broadcasted_iota(jnp.int32, (rows, count), 1)
            query_pos = first + lax.broadcasted_iota(jnp.int32, (rows, count), 0)
            low_wide = jnp.concatenate([low] * (count // HD), axis=1)
            allowed = (key_pos <= query_pos) & (key_pos >= low_wide)
            shaped = raw.reshape(group, rows, count) * scale
            return jnp.where(allowed[None], shaped, -1e30).reshape(group * rows, count)

        def folded(piece, weights):
            return jnp.dot(
                weights.astype(jnp.bfloat16), piece[1], preferred_element_type=jnp.float32
            )

        def by_lane(weights):
            return sum(weights[:, c : c + HD] for c in range(0, weights.shape[1], HD))

        order = [side] + [i for i in range(len(pieces)) if i != side]
        for place, index in enumerate(order):
            piece, base = pieces[index], bases[index]
            count = piece.shape[1]
            if place == 0:
                scores = scored(piece, base)
                peak = jnp.max(scores, axis=1, keepdims=True)
                weights = jnp.exp2(scores - peak)
                top[...] = jnp.broadcast_to(peak, top.shape)
                total[...] = by_lane(weights)
                mixed[...] = folded(piece, weights)
                continue

            @pl.when((base <= first) & (base + count > lowest))
            def _():
                scores = scored(piece, base)
                before = top[...]
                peak = jnp.maximum(before, jnp.max(scores, axis=1, keepdims=True))
                weights = jnp.exp2(scores - jnp.concatenate([peak] * (count // HD), axis=1))
                rescale = jnp.exp2(before - peak)
                top[...] = peak
                total[...] = total[...] * rescale + by_lane(weights)
                mixed[...] = mixed[...] * rescale + folded(piece, weights)

        summed = jnp.sum(total[...], axis=1, keepdims=True)
        result = (mixed[...] / summed).astype(out.dtype)
        for inner in range(rows // BLOCK):
            slot = slots[side * (rows // BLOCK) + inner]
            for g in range(group):
                start = g * rows + inner * BLOCK
                out[slot, :, pl.ds(g * HD, HD)] = result[start : start + BLOCK]


def attention(group, scalars, lows, own_queries, other_queries, pieces, blocks):
    rows = own_queries.shape[0]
    vmem = pl.BlockSpec(memory_space=pltpu.VMEM)
    smem = pl.BlockSpec(memory_space=pltpu.SMEM)
    operands = (*scalars, lows, own_queries, other_queries, *pieces)
    tall = (group * rows, HD)
    keys_seen = len(pieces) * rows
    return pl.pallas_call(
        functools.partial(attend, group),
        out_shape=jax.ShapeDtypeStruct((blocks, BLOCK, group * HD), jnp.bfloat16),
        in_specs=[smem] * len(scalars) + [vmem] * (len(operands) - len(scalars)),
        out_specs=vmem,
        scratch_shapes=[pltpu.VMEM(tall, jnp.float32)] * 3,
        compiler_params=pltpu.CompilerParams(vmem_limit_bytes=24 * 1024 * 1024),
        cost_estimate=pl.CostEstimate(
            flops=24 * blocks * BLOCK * group * HD * keys_seen // 2,
            bytes_accessed=4 * rows * group * HD * 4,
            transcendentals=blocks * BLOCK * group * keys_seen // 2,
        ),
    )(*operands)


def local(queries, keys, values, lengths, home):
    rows, query_cols = queries.shape
    kv_heads = keys.shape[1] // HD
    group = query_cols // HD // kv_heads
    half_heads = kv_heads // 2
    blocks_dev = rows // BLOCK
    blocks = 2 * blocks_dev
    seq = lax.axis_size("seq")
    tokens = seq * rows
    most_len = min(tokens // 2, 4096)
    depth = min(-(-(min(WINDOW, most_len) - 1) // (2 * rows)), seq // 2 - 1)
    me = lax.axis_index("seq")
    other = me ^ 1
    parity = me % 2

    def halves(array):
        width = array.shape[1] // 2
        low, high = array[:, :width], array[:, width:]
        return jnp.where(parity == 0, low, high), jnp.where(parity == 0, high, low)

    def by_head(array):
        return [array[:, h * HD : (h + 1) * HD] for h in range(half_heads)]

    keys_mine, keys_give = halves(keys)
    values_mine, values_give = halves(values)
    own_kv = [jnp.stack(kv) for kv in zip(by_head(keys_mine), by_head(values_mine))]
    give_kv = [jnp.stack(kv) for kv in zip(by_head(keys_give), by_head(values_give))]
    queries_mine, queries_give = halves(queries)
    wide = group * HD

    own_pos = me * rows + jnp.arange(rows, dtype=jnp.int32)
    other_pos = other * rows + jnp.arange(rows, dtype=jnp.int32)
    positions = jnp.concatenate([own_pos, other_pos])
    low = jnp.maximum(doc_first_of(lengths, positions), positions - (WINDOW - 1))
    lows = jnp.broadcast_to(low[:, None], (2 * rows, HD))
    firsts = low[::BLOCK]
    bases = jnp.stack(
        [(device - 2 * back) * rows for back in range(depth + 1) for device in (me, other)]
    ).astype(jnp.int32)
    group_home = lax.dynamic_slice_in_dim(home, me // 2 * blocks, blocks, 0)
    same = group_home[:, None] == group_home[None, :]
    earlier = jnp.arange(blocks)[None, :] < jnp.arange(blocks)[:, None]
    rank = jnp.sum((same & earlier).astype(jnp.int32), axis=1)
    slot = jnp.where(group_home == me, rank, blocks_dev + rank).astype(jnp.int32)
    slots = jnp.where(parity == 0, slot, jnp.roll(slot, blocks_dev))
    ids = jnp.arange(blocks, dtype=jnp.int32)

    outs = []
    pieces = []
    asked = []
    mine = jnp.stack(own_kv)
    theirs = swap(jnp.stack(give_kv))
    found = [mine, theirs]
    for _ in range(depth):
        mine, theirs = hop_back(mine, 1), hop_back(theirs, 1)
        found += [mine, theirs]
    for h in range(half_heads):
        pieces.append([piece[h] for piece in found])
        asked.append(swap(queries_give[:, h * wide : (h + 1) * wide]))
    for h in range(half_heads):
        result = attention(
            group,
            (bases, slots, firsts, ids),
            lows,
            queries_mine[:, h * wide : (h + 1) * wide],
            asked[h],
            pieces[h],
            blocks,
        )
        kept = result[:blocks_dev].reshape(rows, wide)
        got = swap(result[blocks_dev:].reshape(rows, wide))
        outs.append((kept, got))
    kept = jnp.concatenate([pair[0] for pair in outs], axis=1)
    got = jnp.concatenate([pair[1] for pair in outs], axis=1)
    return jnp.where(
        parity == 0,
        jnp.concatenate([kept, got], axis=1),
        jnp.concatenate([got, kept], axis=1),
    )


def solution(mesh):
    placed = (
        P(("pack", "seq"), None),
        P(("pack", "seq"), None),
        P(("pack", "seq"), None),
        P("pack"),
        P("pack"),
    )
    return jax.shard_map(
        local, mesh=mesh, in_specs=placed, out_specs=P(("pack", "seq"), None), check_vma=False
    )
```
